32 devices in a mesh: dp: 8 (over z, y), tensor: 4 (over x, core).
Axes of the slice: x: 2, y: 2, z: 4, core: 2. Of those that a mesh axis runs over, the one named last changes fastest.
Arguments:
- block_input: bfloat16 [8192, 2048], P('dp'), may hold values from -6 to 6
- ln_gain: float32 [2048], replicated, may hold values from 0.5 to 1.5
- ln_bias: float32 [2048], replicated, may hold values from -3 to 3
- qkv_weight: bfloat16 [2048, 3, 2048], P(None, None, 'tensor'), may hold values from -0.125 to 0.125
- qkv_bias: float32 [3, 2048], P(None, 'tensor'), may hold values from -13 to 13
- dense_weight: bfloat16 [2048, 2048], P(None, 'tensor'), may hold values from -0.375 to 0.375
- dense_bias: float32 [2048], replicated, may hold values from -3 to 3
- fc1_weight: bfloat16 [2048, 8192], P(None, 'tensor'), may hold values from -0.125 to 0.125
- fc1_bias: float32 [8192], P('tensor'), may hold values from -3 to 3
- fc2_weight: bfloat16 [2048, 8192], P(None, 'tensor'), may hold values from -0.0625 to 0.0625
- fc2_bias: float32 [2048], replicated, may hold values from -3 to 3
- cotangent: bfloat16 [8192, 2048], P('dp'), may hold values from -6 to 6
Outputs:
- block_output: bfloat16 [8192, 2048], P('dp')
- grad_input: bfloat16 [8192, 2048], P('dp')
- grad_ln_gain: float32 [2048], replicated
- grad_ln_bias: float32 [2048], replicated
- grad_qkv_weight: float32 [2048, 3, 2048], P('dp', None, 'tensor')
- grad_qkv_bias: float32 [3, 2048], P(None, 'tensor')
- grad_dense_weight: float32 [2048, 2048], P('dp', 'tensor')
- grad_dense_bias: float32 [2048], replicated
- grad_fc1_weight: float32 [2048, 8192], P('dp', 'tensor')
- grad_fc1_bias: float32 [8192], P('tensor')
- grad_fc2_weight: float32 [2048, 8192], P('dp', 'tensor')
- grad_fc2_bias: float32 [2048], replicated
The draws below stay inside these ranges and needn't reach their ends.
All inputs are finite; a program needn't handle non-finite values.
Results may differ from the reference program's by a relative error of at most 0.03.
The reference program's roundings to bfloat16 on the way count: a program that leaves them out, or rounds other values in their place, can miss the bound.
Values may be sent and summed in bfloat16 or wider, within the bound.
No kernel may reach another device: no remote copies, remote signals or barrier semaphores. Data moves between devices by JAX's collectives and lax.ppermute only.
A program may use at most 320 MiB of HBM per device.

```python
import math
import jax
import jax.numpy as jnp
from jax import lax

D = 2048
HEADS = 32
HEAD_DIM = 64
ROT_DIM = 32
FF = 8192
SEQ_LEN = 256
TOKENS = 8192


def draw_qkv_bias(key, part):
    drawn = jnp.clip(jax.random.normal(jax.random.fold_in(key, 1), (3, D), jnp.float32) * 0.5, -2.0, 2.0)
    return drawn


def strengthened(values, rng, source, target, blocks, factor):
    def block_of(dim):
        return (jnp.arange(values.shape[dim]) // (values.shape[dim] // blocks)).reshape((-1,) + (1,) * (values.ndim - 1 - dim))

    first = jax.random.permutation(rng, blocks)[block_of(target)]
    second = (block_of(target) + blocks // 2) % blocks
    return jnp.where((block_of(source) == first) | (block_of(source) == second), factor * values, values)


def block_levels(key, extent, shards, least, top_value):
    level = 1.0
    for position, parts in shards:
        steps = jax.random.uniform(jax.random.fold_in(jax.random.fold_in(key, 6), position), (parts,), jnp.float32, least / len(shards), top_value / len(shards))
        level = level * jnp.repeat(jnp.exp(steps), extent[position] // parts).reshape((-1,) + (1,) * (len(extent) - 1 - position))
    return level


def noise(rng, dims, deviation, bound, cuts=(), kind=jnp.bfloat16):
    result = jax.random.normal(rng, dims, jnp.float32) * deviation
    if len(cuts) > 0:
        result = block_levels(rng, dims, cuts, -0.22, 0.18) * result
    return jnp.clip(result, min=-bound, max=bound).astype(kind)


def gaussian_with(key, extent, scale, most, cuts, heavy, kind=jnp.bfloat16):
    entries = scale * jax.random.normal(key, extent, jnp.float32)
    if cuts:
        entries = entries * block_levels(key, extent, cuts, -0.22, 0.18)
    return jnp.clip(strengthened(entries, jax.random.fold_in(key, 3), *heavy), -most, most).astype(kind)


def setup_inputs(seed: int = 0) -> dict:
    keys = jax.random.split(jax.random.key(seed), 13)
    return {
        "block_input": gaussian_with(keys[0], (TOKENS, D), 1.0, 6.0, ((0, 8),), (0, 1, 8, 2.0)),
        "ln_gain": jnp.clip(1.0 + 0.1 * jax.random.normal(keys[1], (D,), jnp.float32), 0.5, 1.5),
        "ln_bias": noise(keys[2], (D,), 0.5, 3.0, (), jnp.float32),
        "qkv_weight": noise(keys[3], (D, 3, D), D ** -0.5, 0.125, ((2, 4),)),
        "qkv_bias": draw_qkv_bias(jax.random.fold_in(keys[12], 71), 0),
        "dense_weight": noise(keys[5], (D, D), (D // 8) ** -0.5, 0.375, ((1, 4),)),
        "dense_bias": noise(keys[6], (D,), 0.5, 3.0, (), jnp.float32),
        "fc1_weight": noise(keys[7], (D, FF), D ** -0.5, 0.125, ((1, 4),)),
        "fc1_bias": noise(keys[8], (FF,), 0.5, 3.0, ((0, 4),), jnp.float32),
        "fc2_weight": noise(keys[9], (D, FF), FF ** -0.5, 0.0625, ((1, 4),)),
        "fc2_bias": noise(keys[10], (D,), 0.5, 3.0, (), jnp.float32),
        "cotangent": gaussian_with(keys[11], (TOKENS, D), 1.0, 6.0, ((0, 8),), (0, 1, 8, 2.0)),
    }


NORM_EPS = 1e-05
GELU_COEF = 0.7978845608028654
CUBIC_COEF = 0.044715

def gelu_value(preact):
    return 0.5 * preact * (1.0 + jnp.tanh(GELU_COEF * (preact + CUBIC_COEF * preact * preact * preact)))

def gelu_slope(preact):
    tangent = jnp.tanh(GELU_COEF * (preact + CUBIC_COEF * preact * preact * preact))
    return 0.5 * (1.0 + tangent) + 0.5 * preact * (1.0 - tangent * tangent) * GELU_COEF * (1.0 + 3.0 * CUBIC_COEF * preact * preact)

def rotary_tables(seq_len, rot_dim):
    half_dim = rot_dim // 2
    frequency = 10000.0 ** (-2.0 * jnp.arange(half_dim, dtype=jnp.float32) / rot_dim)
    angles = jnp.arange(seq_len, dtype=jnp.float32)[:, None] * frequency[None, :]
    return (jnp.cos(angles), jnp.sin(angles))

def rotate(values, cosine, sine_table, direction):
    half_dim = cosine.shape[-1]
    first_half = values[..., :half_dim]
    second_half = values[..., half_dim:2 * half_dim]
    cos_part = cosine[:, None, :]
    sin_part = direction * sine_table[:, None, :]
    return jnp.concatenate([first_half * cos_part - second_half * sin_part, second_half * cos_part + first_half * sin_part, values[..., 2 * half_dim:]], axis=-1)

def masked_scores(query_b, key_b):
    scores = jnp.einsum('sqhe,skhe->shqk', query_b.astype(jnp.float32), key_b.astype(jnp.float32)) * HEAD_DIM ** (-0.5)
    length = query_b.shape[1]
    row_pos = lax.broadcasted_iota(jnp.int32, (length, length), 0)
    col_pos = lax.broadcasted_iota(jnp.int32, (length, length), 1)
    return jnp.where(col_pos <= row_pos, scores, -1e+30)

def reference(block_input, ln_gain, ln_bias, qkv_weight, qkv_bias, dense_weight, dense_bias, fc1_weight, fc1_bias, fc2_weight, fc2_bias, cotangent):
    block_seqs = math.gcd(TOKENS // SEQ_LEN, max(1, 4096 // SEQ_LEN))
    block_rows = block_seqs * SEQ_LEN
    block_count = TOKENS // block_rows
    qkv_flat = qkv_weight.reshape(D, 3 * D)
    cosine, sine_table = rotary_tables(SEQ_LEN, ROT_DIM)
    score_scale = HEAD_DIM ** (-0.5)

    def one_block(totals, pieces):
        rows_in, rows_cot = pieces
        input_float = rows_in.astype(jnp.float32)
        row_mean = lax.optimization_barrier(jnp.mean(input_float, axis=1, keepdims=True))
        centered = input_float - row_mean
        inv_std = lax.rsqrt(lax.optimization_barrier(jnp.mean(centered * centered, axis=1, keepdims=True)) + NORM_EPS)
        normed = centered * inv_std
        hidden_in = (normed * ln_gain + ln_bias).astype(jnp.bfloat16)
        projected = jnp.dot(hidden_in, qkv_flat, preferred_element_type=jnp.float32).reshape(block_rows, 3, D) + qkv_bias

        def heads_of(which_part):
            return projected[:, which_part].reshape(block_seqs, SEQ_LEN, HEADS, HEAD_DIM)
        query_b = rotate(heads_of(0), cosine, sine_table, 1.0).astype(jnp.bfloat16)
        key_b = rotate(heads_of(1), cosine, sine_table, 1.0).astype(jnp.bfloat16)
        value_b = heads_of(2).astype(jnp.bfloat16)
        scores = masked_scores(query_b, key_b)
        row_max = lax.optimization_barrier(jnp.max(scores, axis=-1, keepdims=True))
        log_total = row_max + jnp.log(lax.optimization_barrier(jnp.sum(jnp.exp(scores - row_max), axis=-1, keepdims=True)))
        probs_f = jnp.exp(scores - log_total)
        probs_b = probs_f.astype(jnp.bfloat16)
        context = jnp.einsum('shqk,skhe->sqhe', probs_b.astype(jnp.float32), value_b.astype(jnp.float32)).reshape(block_rows, D).astype(jnp.bfloat16)
        attn_part = jnp.dot(context, dense_weight.T, preferred_element_type=jnp.float32)
        preact = jnp.dot(hidden_in, fc1_weight, preferred_element_type=jnp.float32) + fc1_bias
        activated = gelu_value(preact).astype(jnp.bfloat16)
        mlp_part = jnp.dot(activated, fc2_weight.T, preferred_element_type=jnp.float32)
        block_output = (input_float + attn_part + mlp_part + dense_bias + fc2_bias).astype(jnp.bfloat16)
        grad_out = rows_cot.astype(jnp.float32)
        grad_out_bias = lax.optimization_barrier(jnp.sum(grad_out, axis=0))
        grad_fc2 = jnp.dot(rows_cot.T, activated, preferred_element_type=jnp.float32)
        grad_dense = jnp.dot(rows_cot.T, context, preferred_element_type=jnp.float32)
        grad_preact = (jnp.dot(rows_cot, fc2_weight, preferred_element_type=jnp.float32) * gelu_slope(preact)).astype(jnp.bfloat16)
        grad_fc1 = jnp.dot(hidden_in.T, grad_preact, preferred_element_type=jnp.float32)
        grad_fc1_bias = lax.optimization_barrier(jnp.sum(grad_preact.astype(jnp.float32), axis=0))
        grad_context = jnp.dot(rows_cot, dense_weight, preferred_element_type=jnp.float32).astype(jnp.bfloat16)
        grad_ctx_heads = grad_context.reshape(block_seqs, SEQ_LEN, HEADS, HEAD_DIM).astype(jnp.float32)
        ctx_heads = context.reshape(block_seqs, SEQ_LEN, HEADS, HEAD_DIM).astype(jnp.float32)
        row_delta = lax.optimization_barrier(jnp.sum(grad_ctx_heads * ctx_heads, axis=-1))
        grad_value = jnp.einsum('shqk,sqhe->skhe', probs_b.astype(jnp.float32), grad_ctx_heads)
        grad_probs = jnp.einsum('sqhe,skhe->shqk', grad_ctx_heads, value_b.astype(jnp.float32))
        grad_scores = (probs_f * (grad_probs - jnp.transpose(row_delta, (0, 2, 1))[..., None])).astype(jnp.bfloat16)
        grad_query = jnp.einsum('shqk,skhe->sqhe', grad_scores.astype(jnp.float32), key_b.astype(jnp.float32)) * score_scale
        grad_key = jnp.einsum('shqk,sqhe->skhe', grad_scores.astype(jnp.float32), query_b.astype(jnp.float32)) * score_scale
        grad_qkv = jnp.stack([rotate(grad_query, cosine, sine_table, -1.0).reshape(block_rows, D), rotate(grad_key, cosine, sine_table, -1.0).reshape(block_rows, D), grad_value.reshape(block_rows, D)], axis=1).astype(jnp.bfloat16)
        grad_qkv_flat = grad_qkv.reshape(block_rows, 3 * D)
        grad_qkv_weight = jnp.dot(hidden_in.T, grad_qkv_flat, preferred_element_type=jnp.float32).reshape(D, 3, D)
        grad_qkv_bias = lax.optimization_barrier(jnp.sum(grad_qkv.astype(jnp.float32), axis=0))
        grad_hidden = jnp.dot(grad_qkv_flat, qkv_flat.T, preferred_element_type=jnp.float32) + jnp.dot(grad_preact, fc1_weight.T, preferred_element_type=jnp.float32)
        grad_gain = lax.optimization_barrier(jnp.sum(grad_hidden * normed, axis=0))
        grad_shift = lax.optimization_barrier(jnp.sum(grad_hidden, axis=0))
        scaled = grad_hidden * ln_gain
        mean_one = lax.optimization_barrier(jnp.mean(scaled, axis=1, keepdims=True))
        mean_two = lax.optimization_barrier(jnp.mean(scaled * normed, axis=1, keepdims=True))
        grad_rows = (grad_out + inv_std * (scaled - mean_one - normed * mean_two)).astype(jnp.bfloat16)
        additions = (grad_gain, grad_shift, grad_qkv_weight, grad_qkv_bias, grad_dense, grad_out_bias, grad_fc1, grad_fc1_bias, grad_fc2)
        new_totals = tuple((old + extra for old, extra in zip(totals, additions)))
        return (new_totals, (block_output, grad_rows))
    start_totals = (jnp.zeros((D,), jnp.float32), jnp.zeros((D,), jnp.float32), jnp.zeros((D, 3, D), jnp.float32), jnp.zeros((3, D), jnp.float32), jnp.zeros((D, D), jnp.float32), jnp.zeros((D,), jnp.float32), jnp.zeros((D, FF), jnp.float32), jnp.zeros((FF,), jnp.float32), jnp.zeros((D, FF), jnp.float32))
    totals, (outputs, input_grads) = lax.scan(one_block, start_totals, (block_input.reshape(block_count, block_rows, D), cotangent.reshape(block_count, block_rows, D)))
    grad_gain, grad_shift, grad_qkv_weight, grad_qkv_bias, grad_dense, grad_out_bias, grad_fc1, grad_fc1_bias, grad_fc2 = totals
    return (outputs.reshape(TOKENS, D), input_grads.reshape(TOKENS, D), grad_gain, grad_shift, grad_qkv_weight, grad_qkv_bias, grad_dense, grad_out_bias, grad_fc1, grad_fc1_bias, grad_fc2, grad_out_bias)
```

```python
import functools

import jax
import jax.numpy as jnp
from jax import lax
from jax.experimental import pallas as pl
from jax.experimental.pallas import tpu as pltpu
from jax.sharding import PartitionSpec as P

HEAD_DIM = 64
ROT_DIM = 32
SEQ_LEN = 256
LANES = 128

NORM_EPS = 1e-05
GELU_COEF = 0.7978845608028654
CUBIC_COEF = 0.044715


BF16, F32 = jnp.bfloat16, jnp.float32
ANYWHERE = pl.BlockSpec(memory_space=pl.ANY)


def product(left, right, left_dim, right_dim):
    return lax.dot_general(
        left, right, (((left_dim,), (right_dim,)), ((), ())), preferred_element_type=F32
    )


def fixed(*shape):
    return pl.BlockSpec(shape, lambda *_: (0,) * len(shape))


def shape_of(*shape, kind=BF16):
    return jax.ShapeDtypeStruct(shape, kind)


class Line:
    def __init__(self):
        self.last = None

    def call(self, body, grid, inputs, outputs, name, flops, scalars=(), scratch=(), alias=None):
        arrays, specs = [a for a, _ in inputs], [s for _, s in inputs]
        taken = len(arrays)
        extra = [] if self.last is None else [self.last]

        def kernel(*refs):
            first = len(scalars)
            body(*refs[: first + taken], *refs[first + taken + len(extra) :])

        moved = sum(a.size * a.dtype.itemsize for a in arrays)
        moved += sum(s.size * s.dtype.itemsize for s, _ in outputs)
        results = pl.pallas_call(
            kernel,
            grid_spec=pltpu.PrefetchScalarGridSpec(
                num_scalar_prefetch=len(scalars),
                grid=grid,
                in_specs=specs + [ANYWHERE] * len(extra),
                out_specs=[s for _, s in outputs],
                scratch_shapes=scratch,
            ),
            out_shape=[s for s, _ in outputs],
            input_output_aliases=alias or {},
            compiler_params=pltpu.CompilerParams(vmem_limit_bytes=56 << 20),
            cost_estimate=pl.CostEstimate(flops=flops, bytes_accessed=moved, transcendentals=0),
            name=name,
        )(*scalars, *arrays, *extra)
        self.last = results[0]
        return results


def norm_body(x_ref, cot_ref, gain_ref, bias_ref, hid_ref, hid_t_ref, cot_t_ref, sum_ref):
    x = x_ref[...].astype(F32)
    mean = jnp.mean(x, axis=1, keepdims=True)
    centered = x - mean
    inv_std = lax.rsqrt(jnp.mean(centered * centered, axis=1, keepdims=True) + NORM_EPS)
    hidden = (centered * inv_std * gain_ref[...] + bias_ref[...]).astype(BF16)
    hid_ref[...] = hidden
    hid_t_ref[...] = hidden.T
    cot_t_ref[...] = cot_ref[...].T

    @pl.when(pl.program_id(0) == 0)
    def _():
        sum_ref[...] = jnp.zeros_like(sum_ref)

    sum_ref[...] += jnp.sum(cot_ref[...].astype(F32), axis=0, keepdims=True)


def norm(line, x, cot, gain, bias):
    rows, width = x.shape
    tile = min(rows, 256)
    by_row = pl.BlockSpec((tile, width), lambda i: (i, 0))
    by_col = pl.BlockSpec((width, tile), lambda i: (0, i))
    return line.call(
        norm_body, (rows // tile,),
        [(x, by_row), (cot, by_row), (gain[None], fixed(1, width)), (bias[None], fixed(1, width))],
        [
            (shape_of(rows, width), by_row),
            (shape_of(width, rows), by_col),
            (shape_of(width, rows), by_col),
            (shape_of(1, width, kind=F32), fixed(1, width)),
        ],
        "norm", 20 * x.size,
    )


def feed_body(hidden_ref, cot_ref, w1_ref, b1_ref, w2_ref, act_ref, grad_ref, sum_ref):
    rows = hidden_ref.shape[0]
    step = min(rows, 256)
    total = jnp.zeros(sum_ref.shape, F32)
    for start in range(0, rows, step):
        here = pl.ds(start, step)
        u = product(hidden_ref[here, :], w1_ref[...], 1, 0) + b1_ref[...]
        back = product(cot_ref[here, :], w2_ref[...], 1, 0)
        square = u * u
        th = jnp.tanh(GELU_COEF * (u + CUBIC_COEF * square * u))
        act_ref[here, :] = (0.5 * u * (1.0 + th)).astype(BF16)
        slope = 0.5 * (1.0 + th) + 0.5 * u * (1.0 - th * th) * GELU_COEF * (
            1.0 + 3.0 * CUBIC_COEF * square
        )
        grad = (back * slope).astype(BF16)
        grad_ref[here, :] = grad
        total += jnp.sum(grad.astype(F32), axis=0, keepdims=True)
    sum_ref[...] = total


def feed(line, hidden, cot, w1, b1, w2, part, parts):
    rows, width = hidden.shape
    local = w1.shape[1] // parts
    step = min(local, 256)
    first = part * (local // step)
    weight = pl.BlockSpec((width, step), lambda i: (0, i + first))
    result = pl.BlockSpec((rows, step), lambda i: (0, i))
    return line.call(
        feed_body, (local // step,),
        [
            (hidden, fixed(rows, width)),
            (cot, fixed(rows, width)),
            (w1, weight),
            (b1[None], pl.BlockSpec((1, step), lambda i: (0, i + first))),
            (w2, weight),
        ],
        [
            (shape_of(rows, local), result),
            (shape_of(rows, local), result),
            (shape_of(1, local, kind=F32), pl.BlockSpec((1, step), lambda i: (0, i))),
        ],
        f"feed{part}", 4 * rows * width * local,
    )


def rotary_rows(seq_len):
    half = ROT_DIM // 2
    frequency = 10000.0 ** (-2.0 * jnp.arange(half, dtype=F32) / ROT_DIM)
    angles = jnp.arange(seq_len, dtype=F32)[:, None] * frequency[None, :]
    cosine, sine = jnp.cos(angles), jnp.sin(angles)
    rest = HEAD_DIM - ROT_DIM
    ones, none = jnp.ones((seq_len, rest), F32), jnp.zeros((seq_len, rest), F32)
    blank = jnp.zeros((seq_len, half), F32)
    heads = LANES // HEAD_DIM
    keep = jnp.tile(jnp.concatenate([cosine, cosine, ones], axis=1), (1, heads))
    from_right = jnp.tile(jnp.concatenate([-sine, blank, none], axis=1), (1, heads))
    from_left = jnp.tile(jnp.concatenate([blank, sine, none], axis=1), (1, heads))
    return jnp.stack([keep, from_right, from_left])


def turned(values, tables, sign):
    half = ROT_DIM // 2
    right = pltpu.roll(values, LANES - half, 1)
    left = pltpu.roll(values, half, 1)
    return values * tables[0] + sign * (right * tables[1] + left * tables[2])


def attention_body(
    tables_ref, hidden_ref, cot_ref, wqkv_ref, bias_ref, dense_ref,
    ctx_ref, grads_ref, sums_ref, q_s, k_s, v_s, g_s,
):
    rows, width = ctx_ref.shape
    scale = HEAD_DIM ** (-0.5)
    groups = width // LANES
    seqs = rows // SEQ_LEN
    for kind, store in ((0, q_s), (1, k_s), (2, v_s)):
        for seq in range(seqs):
            here = pl.ds(seq * SEQ_LEN, SEQ_LEN)
            raw = product(hidden_ref[here, :], wqkv_ref[kind], 1, 0) + bias_ref[kind][None, :]
            for group in range(groups):
                lanes = slice(group * LANES, (group + 1) * LANES)
                part = raw[:, lanes]
                if kind < 2:
                    part = turned(part, tables_ref, 1.0)
                store[here, lanes] = part.astype(BF16)
    for seq in range(seqs):
        here = pl.ds(seq * SEQ_LEN, SEQ_LEN)
        g_s[here, :] = product(cot_ref[here, :], dense_ref[...], 1, 0).astype(BF16)
    sums_ref[...] = jnp.zeros_like(sums_ref)
    lane = lax.broadcasted_iota(jnp.int32, (SEQ_LEN, LANES), 1)
    row = lax.broadcasted_iota(jnp.int32, (SEQ_LEN, SEQ_LEN), 0)
    col = lax.broadcasted_iota(jnp.int32, (SEQ_LEN, SEQ_LEN), 1)

    @pl.loop(0, seqs)
    def _(seq):
        here = pl.ds(pl.multiple_of(seq * SEQ_LEN, SEQ_LEN), SEQ_LEN)
        for group in range(groups):
            lanes = slice(group * LANES, (group + 1) * LANES)
            q, k, v, g = q_s[here, lanes], k_s[here, lanes], v_s[here, lanes], g_s[here, lanes]
            ctx = jnp.zeros((SEQ_LEN, LANES), F32)
            blank = jnp.zeros_like(q)
            saved = []
            for head in range(LANES // HEAD_DIM):
                mine = (lane // HEAD_DIM) == head
                scores = product(jnp.where(mine, q, blank), k, 1, 1) * scale
                scores = jnp.where(col <= row, scores, -1e30)
                top = jnp.max(scores, axis=-1, keepdims=True)
                grown = jnp.exp(scores - top)
                probs = grown * (1.0 / jnp.sum(grown, axis=-1, keepdims=True))
                probs_b = probs.astype(BF16)
                ctx += product(probs_b, jnp.where(mine, v, blank), 1, 0)
                saved.append((mine, probs, probs_b))
            ctx_b = ctx.astype(BF16)
            ctx_ref[here, lanes] = ctx_b
            both = g.astype(F32) * ctx_b.astype(F32)
            dq = jnp.zeros((SEQ_LEN, LANES), F32)
            dk, dv = dq, dq
            for mine, probs, probs_b in saved:
                g_mine = jnp.where(mine, g, blank)
                delta = jnp.sum(jnp.where(mine, both, 0.0), axis=-1, keepdims=True)
                dprobs = product(g_mine, v, 1, 1)
                dscores = (probs * (dprobs - delta)).astype(BF16)
                dv += product(probs_b, g_mine, 0, 0)
                dq += product(dscores, jnp.where(mine, k, blank), 1, 0)
                dk += product(dscores, jnp.where(mine, q, blank), 0, 0)
            dq = turned(dq * scale, tables_ref, -1.0).astype(BF16)
            dk = turned(dk * scale, tables_ref, -1.0).astype(BF16)
            dv = dv.astype(BF16)
            for kind, part in ((0, dq), (1, dk), (2, dv)):
                grads_ref[kind, here, lanes] = part
                sums_ref[kind : kind + 1, lanes] += jnp.sum(
                    part.astype(F32), axis=0, keepdims=True
                )


def attention(line, hidden, cot, wqkv, bias, dense, part, parts):
    rows, width = hidden.shape
    local = dense.shape[1] // parts
    step = min(local, 2 * LANES)
    first = part * (local // step)
    return line.call(
        attention_body, (local // step,),
        [
            (rotary_rows(SEQ_LEN), fixed(3, SEQ_LEN, LANES)),
            (hidden, fixed(rows, width)),
            (cot, fixed(rows, width)),
            (wqkv, pl.BlockSpec((3, width, step), lambda i: (0, 0, i + first))),
            (bias, pl.BlockSpec((3, step), lambda i: (0, i + first))),
            (dense, pl.BlockSpec((width, step), lambda i: (0, i + first))),
        ],
        [
            (shape_of(rows, local), pl.BlockSpec((rows, step), lambda i: (0, i))),
            (shape_of(3, rows, local), pl.BlockSpec((3, rows, step), lambda i: (0, 0, i))),
            (shape_of(3, local, kind=F32), pl.BlockSpec((3, step), lambda i: (0, i))),
        ],
        f"attention{part}", 8 * rows * width * local + 14 * rows * SEQ_LEN * local,
        scratch=[pltpu.VMEM((rows, step), BF16)] * 4,
    )


def ring_order(size):
    if size % 2:
        return list(range(size))
    return list(range(0, size, 2)) + list(range(size - 1, 0, -2))


class Ring:
    def __init__(self, line, dp, tensor):
        self.line, self.size = line, dp
        order = ring_order(dp)
        place = [order.index(i) for i in range(dp)]
        turns = [-1 if tensor % 2 == 0 and t % 2 else 1 for t in range(tensor)]
        self.pairs = [
            (d * tensor + t, order[(place[d] + turns[t]) % dp] * tensor + t)
            for d in range(dp)
            for t in range(tensor)
        ]
        table = [
            [order[(place[d] - turns[t] * (1 + step)) % dp] for step in range(dp)]
            for d in range(dp)
            for t in range(tensor)
        ]
        me = lax.axis_index("dp") * tensor + lax.axis_index("tensor")
        self.targets = lax.dynamic_index_in_dim(
            jnp.asarray(table, jnp.int32), me, 0, keepdims=False
        )


class Stream:
    def __init__(self, ring, name, pieces):
        self.ring, self.name, self.pieces = ring, name, pieces
        self.step, self.travelling = 0, None

    def hop(self):
        outs = self.compute(BF16)
        self.travelling = lax.ppermute(outs, ("dp", "tensor"), self.ring.pairs)
        self.step += 1

    def compute(self, kind):
        size, step, pieces = self.ring.size, self.step, self.pieces
        rows, width = pieces[0][1].shape
        lefts = []
        for left, _ in pieces:
            if not any(left is other for other in lefts):
                lefts.append(left)
        which = [next(i for i, o in enumerate(lefts) if o is left) for left, _ in pieces]
        block = lefts[0].shape[0] // size
        count = len(pieces)
        tile = min(width, 512)
        has = self.travelling is not None

        def body(targets_ref, *refs):
            left_refs, refs = refs[: len(lefts)], refs[len(lefts) :]
            right_refs, refs = refs[:count], refs[count:]
            out_ref = refs[-1]
            for index in range(count):
                part = product(left_refs[which[index]][...], right_refs[index][...], 1, 0)
                if has:
                    part = part + refs[0][index].astype(F32)
                out_ref[index] = part.astype(out_ref.dtype)

        piece = pl.BlockSpec((count, block, tile), lambda i, t: (0, 0, i))
        inputs = [(l, pl.BlockSpec((block, rows), lambda i, t: (t[step], 0))) for l in lefts]
        inputs += [(r, pl.BlockSpec((rows, tile), lambda i, t: (0, i))) for _, r in pieces]
        if has:
            inputs.append((self.travelling, piece))
        return self.ring.line.call(
            body, (width // tile,), inputs,
            [(shape_of(count, block, width, kind=kind), piece)],
            f"{self.name}{step}", 2 * count * block * rows * width,
            scalars=(self.ring.targets,),
        )[0]

    def finish(self):
        return self.compute(F32)


def half_body(terms, has, half_ref, *refs):
    left_refs, refs = refs[:terms], refs[terms:]
    right_refs, refs = refs[:terms], refs[terms:]
    total = None
    for left_ref, right_ref in zip(left_refs, right_refs):
        lead = left_ref[...], right_ref[...]
        if len(left_ref.shape) == 3:
            pairs = [(left_ref[i], right_ref[i]) for i in range(left_ref.shape[0])]
        else:
            pairs = [lead]
        for left, right in pairs:
            part = product(left, right, 1, 1)
            total = part if total is None else total + part
    if has:
        total = total + refs[0][...].astype(F32)
    refs[-1][...] = total.astype(BF16)


def half_rows(line, half, other, terms, received, name):
    rows = terms[0][0].shape[-2] // 2
    width = terms[0][1].shape[-2]
    tile = min(width, 256)
    row = (lambda h: 1 - h[0]) if other else (lambda h: h[0])
    inputs, flops = [], 0
    for left, _, _ in terms:
        depth = left.shape[-1]
        if left.ndim == 3:
            spec = pl.BlockSpec((left.shape[0], rows, depth), lambda i, h: (0, row(h), 0))
        else:
            spec = pl.BlockSpec((rows, depth), lambda i, h: (row(h), 0))
        inputs.append((left, spec))
        flops += 2 * left.size // 2 * width
    for left, right, at in terms:
        depth = left.shape[-1]
        if right.ndim == 3:
            spec = pl.BlockSpec((right.shape[0], tile, depth), lambda i, h, at=at: (0, i, at))
        else:
            spec = pl.BlockSpec((tile, depth), lambda i, h, at=at: (i, at))
        inputs.append((right, spec))
    if received is not None:
        inputs.append((received, pl.BlockSpec((rows, tile), lambda i, h: (0, i))))
    return line.call(
        functools.partial(half_body, len(terms), received is not None),
        (width // tile,), inputs,
        [(shape_of(rows, width), pl.BlockSpec((rows, tile), lambda i, h: (0, i)))],
        name, flops, scalars=(half,),
    )[0]


def output_body(half_ref, x_ref, mine_ref, far_ref, b1_ref, b2_ref, full_ref, send_ref):
    summed = mine_ref[...].astype(F32) + far_ref[...].astype(F32)
    result = (x_ref[...].astype(F32) + summed + b1_ref[...] + b2_ref[...]).astype(BF16)
    full_ref[...] = result
    send_ref[...] = result


def input_body(
    half_ref, x_ref, cot_ref, mine_ref, far_ref, gain_ref, full_ref, send_ref, sums_ref
):
    x = x_ref[...].astype(F32)
    mean = jnp.mean(x, axis=1, keepdims=True)
    centered = x - mean
    inv_std = lax.rsqrt(jnp.mean(centered * centered, axis=1, keepdims=True) + NORM_EPS)
    normed = centered * inv_std
    grad = mine_ref[...].astype(F32) + far_ref[...].astype(F32)
    scaled = grad * gain_ref[...]
    mean_one = jnp.mean(scaled, axis=1, keepdims=True)
    mean_two = jnp.mean(scaled * normed, axis=1, keepdims=True)
    result = cot_ref[...].astype(F32) + inv_std * (scaled - mean_one - normed * mean_two)
    full_ref[...] = result.astype(BF16)
    send_ref[...] = result.astype(BF16)

    @pl.when(pl.program_id(0) == 0)
    def _():
        sums_ref[...] = jnp.zeros_like(sums_ref)

    sums_ref[0:1] += jnp.sum(grad * normed, axis=0, keepdims=True)
    sums_ref[1:2] += jnp.sum(grad, axis=0, keepdims=True)


def fill_body(half_ref, got_ref, full_ref, out_ref):
    out_ref[...] = got_ref[...]


class Rows:
    def __init__(self, full, half):
        rows, self.width = full.shape
        self.tile = min(rows // 2, 128)
        self.count = rows // 2 // self.tile
        self.full, self.half = full, half

    def whole(self, other=False):
        count = self.count
        if other:
            return pl.BlockSpec((self.tile, self.width), lambda i, h: ((1 - h[0]) * count + i, 0))
        return pl.BlockSpec((self.tile, self.width), lambda i, h: (h[0] * count + i, 0))

    def part(self):
        return pl.BlockSpec((self.tile, self.width), lambda i, h: (i, 0))


def finish_rows(line, body, half, halves, wholes, vectors, sums, name):
    rows = Rows(wholes[0], half)
    width = rows.width
    inputs = [(a, rows.whole()) for a in wholes] + [(a, rows.part()) for a in halves]
    inputs += [(v[None], fixed(1, width)) for v in vectors]
    outputs = [
        (shape_of(*wholes[0].shape), rows.whole()),
        (shape_of(wholes[0].shape[0] // 2, width), rows.part()),
    ]
    if sums:
        outputs.append((shape_of(sums, width, kind=F32), fixed(sums, width)))
    return line.call(
        body, (rows.count,), inputs, outputs, name, 20 * wholes[0].size, scalars=(half,)
    )


def fill(line, half, got, full, name):
    rows = Rows(full, half)
    return line.call(
        fill_body, (rows.count,), [(got, rows.part()), (full, ANYWHERE)],
        [(shape_of(*full.shape), rows.whole(True))],
        name, got.size, scalars=(half,), alias={2: 0},
    )[0]


def shards(
    dp, tensor,
    block_input, ln_gain, ln_bias, qkv_weight, qkv_bias, dense_weight, dense_bias,
    fc1_weight, fc1_bias, fc2_weight, fc2_bias, cotangent,
):
    line = Line()
    wqkv = jnp.transpose(qkv_weight, (1, 0, 2))
    half = (lax.axis_index("tensor") % 2).astype(jnp.int32)[None]
    swap = [(i, i ^ 1) for i in range(tensor)]
    across = [(i, (i + 2) % tensor) for i in range(tensor)]
    ring = Ring(line, dp, tensor)

    hidden, hidden_t, cot_t, out_sum = norm(line, block_input, cotangent, ln_gain, ln_bias)
    act, pre, pre_sum, streams = [], [], [], []
    for part in range(2):
        a, g, s = feed(line, hidden, cotangent, fc1_weight, fc1_bias, fc2_weight, part, 2)
        act.append(a), pre.append(g), pre_sum.append(s)
        streams.append(Stream(ring, f"ff{part}_", [(cot_t, a), (hidden_t, g)]))
        streams[part].hop()
    low, high = streams
    low.hop()
    context, grads, qkv_sum = attention(
        line, hidden, cotangent, wqkv, qkv_bias, dense_weight, 0, 1
    )
    heads = Stream(
        ring, "at_",
        [(hidden_t, grads[0]), (hidden_t, grads[1]), (hidden_t, grads[2]), (cot_t, context)],
    )
    high.hop()
    low.hop()
    heads.hop()
    wide = act[0].shape[1]
    assert wide * 2 == fc2_weight.shape[1]
    forward = [(context, dense_weight, 0), (act[0], fc2_weight, 0), (act[1], fc2_weight, 1)]
    backward = [(grads, wqkv, 0), (pre[0], fc1_weight, 0), (pre[1], fc1_weight, 1)]

    other = half_rows(line, half, True, forward, None, "out_other")
    got = lax.ppermute(other, "tensor", swap)
    high.hop()
    mine = half_rows(line, half, False, forward, got, "out_mine")
    far = lax.ppermute(mine, "tensor", across)
    low.hop()
    heads.hop()
    other = half_rows(line, half, True, backward, None, "in_other")
    got = lax.ppermute(other, "tensor", swap)
    high.hop()
    mine_in = half_rows(line, half, False, backward, got, "in_mine")
    far_in = lax.ppermute(mine_in, "tensor", across)
    low.hop()
    heads.hop()
    high.hop()
    low.hop()
    full, send = finish_rows(
        line, output_body, half, [mine, far], [block_input], [dense_bias, fc2_bias], 0, "output"
    )
    got = lax.ppermute(send, "tensor", swap)
    heads.hop()
    high.hop()
    block_output = fill(line, half, got, full, "output_fill")
    low.hop()
    heads.hop()
    full, send, sums = finish_rows(
        line, input_body, half, [mine_in, far_in], [block_input, cotangent], [ln_gain], 2, "input"
    )
    got = lax.ppermute(send, "tensor", swap)
    sums = sums + lax.ppermute(sums, "tensor", swap)
    high.hop()
    grad_input = fill(line, half, got, full, "input_fill")
    sizes = [pre_sum[0].shape[1], pre_sum[1].shape[1], qkv_sum.size, out_sum.size, sums.size]
    packed = jnp.concatenate(
        [pre_sum[0][0], pre_sum[1][0], qkv_sum.reshape(-1), out_sum[0], sums.reshape(-1)]
    )
    distance = 1
    while distance < dp:
        packed = packed + lax.ppermute(packed, "dp", [(i, i ^ distance) for i in range(dp)])
        distance *= 2
    while low.step < dp - 1 or heads.step < dp - 1 or high.step < dp - 1:
        for stream in (low, heads, high):
            if stream.step < dp - 1:
                stream.hop()
    low_done = low.finish()
    high_done = high.finish()
    heads_done = heads.finish()
    ends = [sum(sizes[: i + 1]) for i in range(len(sizes))]
    fc1_sum = packed[: ends[1]]
    qkv_total = packed[ends[1] : ends[2]].reshape(qkv_sum.shape)
    out_total = packed[ends[2] : ends[3]]
    gain_shift = packed[ends[3] :].reshape(sums.shape)
    return (
        block_output,
        grad_input,
        gain_shift[0],
        gain_shift[1],
        jnp.transpose(heads_done[:3], (1, 0, 2)),
        qkv_total,
        heads_done[3],
        out_total,
        jnp.concatenate([low_done[1], high_done[1]], axis=1),
        fc1_sum,
        jnp.concatenate([low_done[0], high_done[0]], axis=1),
        out_total,
    )


def solution(mesh):
    placed = (
        P("dp", None), P(), P(), P(None, None, "tensor"), P(None, "tensor"),
        P(None, "tensor"), P(), P(None, "tensor"), P("tensor"), P(None, "tensor"),
        P(), P("dp", None),
    )
    given = (
        P("dp", None), P("dp", None), P(), P(), P("dp", None, "tensor"),
        P(None, "tensor"), P("dp", "tensor"), P(), P("dp", "tensor"), P("tensor"),
        P("dp", "tensor"), P(),
    )
    body = functools.partial(shards, mesh.shape["dp"], mesh.shape["tensor"])
    return jax.shard_map(body, mesh=mesh, in_specs=placed, out_specs=given, check_vma=False)
```
